512 devices in a mesh: seq: 32 (over y_lo, z), head: 16 (over x, y_hi, core).
Axes of the slice: x: 4, y: 4 (y_hi: 2, y_lo: 2; y = y_hi * 2 + y_lo), z: 16, core: 2. Of those that a mesh axis runs over, the one named last changes fastest.
Arguments:
- queries: bfloat16 [65536, 2048], P(('seq', 'head')), may hold values from -27 to 27
- key_vectors: bfloat16 [65536, 2048], P(('seq', 'head')), may hold values from -6 to 6
- value_vectors: bfloat16 [65536, 2048], P(('seq', 'head')), may hold values from -6 to 6
- grad_output: bfloat16 [65536, 2048], P(('seq', 'head')), may hold values from -6 to 6
Outputs:
- grad_queries: bfloat16 [65536, 2048], P(('seq', 'head'))
- grad_keys: bfloat16 [65536, 2048], P(('seq', 'head'))
- grad_values: bfloat16 [65536, 2048], P(('seq', 'head'))
The draws below stay inside these ranges and needn't reach their ends.
All inputs are finite; a program needn't handle non-finite values.
Results may differ from the reference program's by a relative error of at most 0.009.
Values may be sent and summed in bfloat16 or wider, within the bound.
A program may use at most 64 MiB of HBM per device.

```python
import jax
import jax.numpy as jnp
from jax import lax

HEADS = 16
HEAD_DIM = 128
D = 2048
WINDOW = 512
TOKENS = 65536


def drawn_pair(key):
    key_query = jax.random.fold_in(key, 11)
    key_key = jax.random.fold_in(key, 12)
    shape = (TOKENS, D)
    query_out = jnp.clip(jax.random.normal(key_query, shape, jnp.float32), -6.0, 6.0)
    key_out = jnp.clip(jax.random.normal(key_key, shape, jnp.float32), -6.0, 6.0)
    return (query_out, key_out)


def draw_queries(key, part):
    return drawn_pair(key)[0].astype(jnp.bfloat16)


def draw_key_vectors(key, part):
    return drawn_pair(key)[1].astype(jnp.bfloat16)


def levels(stream_key, extent, pieces, least, high):
    level = 1.0
    for position, shards_of in pieces:
        steps = jax.random.uniform(jax.random.fold_in(jax.random.fold_in(stream_key, 6), position), (shards_of,), jnp.float32, least / len(pieces), high / len(pieces))
        level = level * jnp.repeat(jnp.exp(steps), extent[position] // shards_of).reshape((-1,) + (1,) * (len(extent) - 1 - position))
    return level


def centred(rng, dims, scale, limit, cuts=(), kind=jnp.bfloat16):
    result = scale * jax.random.normal(rng, dims, jnp.float32)
    if cuts:
        result = result * levels(rng, dims, cuts, -0.22, 0.18)
    return jnp.clip(result, -limit, limit).astype(kind)


def setup_inputs(seed: int = 0) -> dict:
    key_of = jax.random.split(jax.random.key(seed), 5)
    return {
        "queries": draw_queries(jax.random.fold_in(key_of[4], 71), 0),
        "key_vectors": draw_key_vectors(jax.random.fold_in(key_of[4], 71), 0),
        "value_vectors": centred(key_of[2], (TOKENS, D), 1.0, 6.0, ((0, 512),)),
        "grad_output": centred(key_of[3], (TOKENS, D), 1.0, 6.0, ((0, 512),)),
    }


def tile_grads(query_rows, key_rows, value_rows, grad_rows, allowed):
    factor = HEAD_DIM ** -0.5
    best = lax.Precision.HIGHEST
    query_f = query_rows.astype(jnp.float32)
    key_f = key_rows.astype(jnp.float32)
    value_f = value_rows.astype(jnp.float32)
    grad_f = grad_rows.astype(jnp.float32)
    scores = jnp.einsum('rhe,che->hrc', query_f, key_f, precision=best) * factor
    scores = jnp.where(allowed[None], scores, -1e30)
    row_max = jnp.max(scores, axis=-1)
    log_total = row_max + jnp.log(jnp.sum(jnp.exp(scores - row_max[..., None]), axis=-1))
    attn_probs = jnp.exp(scores - log_total[..., None])
    probs_low = lax.optimization_barrier(attn_probs.astype(jnp.bfloat16)).astype(jnp.float32)
    attn_out = jnp.einsum('hrc,che->hre', probs_low, value_f, precision=best)
    row_dots = jnp.sum(jnp.transpose(grad_f, (1, 0, 2)) * attn_out, axis=-1)
    grad_probs = jnp.einsum('rhe,che->hrc', grad_f, value_f, precision=best)
    grad_scores = attn_probs * (grad_probs - row_dots[..., None])
    grad_scores = lax.optimization_barrier(grad_scores.astype(jnp.bfloat16)).astype(jnp.float32)
    grad_query = jnp.einsum('hrc,che->rhe', grad_scores, key_f, precision=best) * factor
    grad_key = jnp.einsum('hrc,rhe->che', grad_scores, query_f, precision=best) * factor
    grad_value = jnp.einsum('hrc,rhe->che', probs_low, grad_f, precision=best)
    return grad_query, grad_key, grad_value


def reference(queries, key_vectors, value_vectors, grad_output):
    token_count = queries.shape[0]
    blocks = token_count // WINDOW
    shape = (token_count, HEADS, HEAD_DIM)
    query_all = queries.reshape(shape)
    grad_all = grad_output.reshape(shape)
    front = jnp.zeros((WINDOW, HEADS, HEAD_DIM), jnp.bfloat16)
    key_all = jnp.concatenate([front, key_vectors.reshape(shape)], axis=0)
    value_all = jnp.concatenate([front, value_vectors.reshape(shape)], axis=0)
    row_ids = jnp.arange(WINDOW, dtype=jnp.int32)[:, None]
    col_ids = jnp.arange(2 * WINDOW, dtype=jnp.int32)[None, :]
    band = (col_ids > row_ids) & (col_ids <= row_ids + WINDOW)

    def one_block(block_index):
        start = (block_index * WINDOW).astype(jnp.int32)
        query_rows = lax.dynamic_slice_in_dim(query_all, start, WINDOW, 0)
        grad_rows = lax.dynamic_slice_in_dim(grad_all, start, WINDOW, 0)
        key_rows = lax.dynamic_slice_in_dim(key_all, start, 2 * WINDOW, 0)
        value_rows = lax.dynamic_slice_in_dim(value_all, start, 2 * WINDOW, 0)
        allowed = band & ((col_ids >= WINDOW) | (block_index > 0))
        grad_query, grad_key, grad_value = tile_grads(query_rows, key_rows, value_rows, grad_rows, allowed)
        return (grad_query.astype(jnp.bfloat16), grad_key[:WINDOW], grad_key[WINDOW:],
                grad_value[:WINDOW], grad_value[WINDOW:])

    grad_query, key_front, key_back, value_front, value_back = lax.map(one_block, jnp.arange(blocks, dtype=jnp.int32))
    grad_key = key_back + jnp.concatenate([key_front[1:], jnp.zeros_like(key_front[:1])], axis=0)
    grad_value = value_back + jnp.concatenate([value_front[1:], jnp.zeros_like(value_front[:1])], axis=0)
    width = HEADS * HEAD_DIM
    return (grad_query.reshape(token_count, width),
            grad_key.reshape(token_count, width).astype(jnp.bfloat16),
            grad_value.reshape(token_count, width).astype(jnp.bfloat16))
```

```python
import functools

import jax
import jax.numpy as jnp
from jax import lax
from jax.experimental import pallas as pl
from jax.experimental.pallas import tpu as pltpu
from jax.sharding import PartitionSpec as P

HEAD_DIM = 128
CHUNK = 256
CHUNKS = 8
HALO = 2
ROWS = 128
SCALE = HEAD_DIM ** (-0.5)
LOG2E = 1.4426950408889634
NEG = -1e30
MESH = pl.DeviceIdType.MESH
K, V, Q, G, DQ, DK, DV = range(7)
NT = (((1,), (1,)), ((), ()))


def kernel(
    q_hbm, k_hbm, v_hbm, g_hbm,
    dq_hbm, dk_hbm, dv_hbm,
    kbuf, vbuf, qbuf, gbuf, kt, probs, dprobs,
    dk_acc, dv_acc, dq_out, dk_out, dv_out, part_k, part_v,
    send_sem, recv_sem, hs_sem, hr_sem,
):
    s = lax.axis_index("seq")
    me = lax.axis_index("head")
    blocks = lax.axis_size("seq")
    chip, core = me // 2, me % 2
    cx, cy = chip // 2, chip % 2
    first = s == 0
    last = s == blocks - 1

    def partner_chip(o):
        return ((cx + o // 2) % 4) * 2 + (cy + o) % 2

    others = [(o, d) for o in range(8) for d in range(2) if (o, d) != (0, 0)]

    def device(o, d):
        return partner_chip(o) * 2 + (core + d) % 2

    barrier = pltpu.get_barrier_semaphore()
    for o, d in others:
        pl.semaphore_signal(barrier, inc=1, device_id=(s, device(o, d)), device_id_type=MESH)

    @pl.when(jnp.logical_not(first))
    def _():
        pl.semaphore_signal(barrier, inc=1, device_id=(s - 1, me), device_id_type=MESH)

    @pl.when(jnp.logical_not(last))
    def _():
        pl.semaphore_signal(barrier, inc=1, device_id=(s + 1, me), device_id_type=MESH)

    inputs = {K: (k_hbm, kbuf, HALO * CHUNK), V: (v_hbm, vbuf, HALO * CHUNK), Q: (q_hbm, qbuf, 0), G: (g_hbm, gbuf, 0)}

    def rows(start, size):
        return pl.ds(pl.multiple_of(start, ROWS), size)

    def local_in(a):
        src, dst, base = inputs[a]
        return pltpu.make_async_copy(
            src.at[:, rows(me * ROWS, HEAD_DIM)], dst.at[rows(base + me * ROWS, ROWS)], recv_sem.at[a, me]
        )

    def remote_in(a, to, source):
        src, dst, base = inputs[a]
        return pltpu.make_async_remote_copy(
            src.at[:, rows(to * HEAD_DIM, HEAD_DIM)],
            dst.at[rows(base + source * ROWS, ROWS)],
            send_sem.at[a, to],
            recv_sem.at[a, source],
            device_id=(s, to),
            device_id_type=MESH,
        )

    for a in (K, V, Q, G):
        local_in(a).start()

    zero = jnp.zeros((HALO * CHUNK, HEAD_DIM), jnp.bfloat16)

    @pl.when(first)
    def _():
        kbuf[: HALO * CHUNK] = zero
        vbuf[: HALO * CHUNK] = zero

    dk_acc[...] = jnp.zeros_like(dk_acc)
    dv_acc[...] = jnp.zeros_like(dv_acc)

    count = 15 + jnp.where(first, 0, 1) + jnp.where(last, 0, 1)
    pl.semaphore_wait(barrier, count)

    for a in (K, V, Q, G):
        for o, d in others:
            remote_in(a, device(o, d), me).start()

    def wait_in(a, o):
        for d in range(2):
            if isinstance(o, int):
                if (o, d) == (0, 0):
                    local_in(a).wait()
                else:
                    remote_in(a, me, device(o, d)).wait_recv()
            else:
                remote_in(a, me, device(o, d)).wait_recv()

    def halo(i, buf):
        return pltpu.make_async_remote_copy(
            buf.at[pl.ds(CHUNKS * CHUNK, HALO * CHUNK)],
            buf.at[pl.ds(0, HALO * CHUNK)],
            hs_sem.at[i],
            hr_sem.at[i],
            device_id=(s + 1, me),
            device_id_type=MESH,
        )

    for i, (a, buf) in enumerate(((K, kbuf), (V, vbuf))):
        for o in range(8):
            wait_in(a, o)

        @pl.when(jnp.logical_not(last))
        def _():
            halo(i, buf).start()

        if a == K:

            @pl.loop(HALO, HALO + CHUNKS)
            def _(b):
                kt[b] = kbuf[rows(b * CHUNK, CHUNK), :].T

    @pl.when(jnp.logical_not(first))
    def _():
        halo(0, kbuf).wait_recv()

    for b in range(HALO):
        kt[b] = kbuf[b * CHUNK : (b + 1) * CHUNK, :].T

    key_ids = lax.broadcasted_iota(jnp.int32, (CHUNK, CHUNK), 0)
    query_ids = lax.broadcasted_iota(jnp.int32, (CHUNK, CHUNK), 1)

    def softmax(c):
        queries = qbuf[rows(c * CHUNK, CHUNK), :]
        top = None
        for b in range(3):
            scores = lax.dot_general(
                kbuf[rows((c + b) * CHUNK, CHUNK), :], queries, NT, preferred_element_type=jnp.float32
            )
            if b == 0:
                scores = jnp.where(key_ids > query_ids, scores, NEG)
            if b == 2:
                scores = jnp.where(key_ids <= query_ids, scores, NEG)
            if b < 2:
                scores = scores + jnp.where(first & (c + b < HALO), NEG, 0.0)
            probs[c, b] = scores
            best = jnp.max(scores, axis=0, keepdims=True)
            top = best if top is None else jnp.maximum(top, best)
        total = None
        for b in range(3):
            e = jnp.exp2((probs[c, b] - top) * (SCALE * LOG2E))
            probs[c, b] = e
            part = jnp.sum(e, axis=0, keepdims=True)
            total = part if total is None else total + part
        inverse = 1.0 / total
        for b in range(3):
            probs[c, b] = probs[c, b] * inverse

    for o in range(8):
        wait_in(Q, o)

    @pl.loop(0, CHUNKS)
    def _(c):
        softmax(c)

    @pl.when(jnp.logical_not(first))
    def _():
        halo(1, vbuf).wait_recv()

    def gradients(c):
        queries = qbuf[rows(c * CHUNK, CHUNK), :]
        grads = gbuf[rows(c * CHUNK, CHUNK), :]
        dots = None
        for b in range(3):
            window = rows((c + b) * CHUNK, CHUNK)
            p = probs[c, b]
            dv_acc[window, :] += jnp.dot(p.astype(jnp.bfloat16), grads, preferred_element_type=jnp.float32)
            dp = lax.dot_general(vbuf[window, :], grads, NT, preferred_element_type=jnp.float32)
            dprobs[b] = dp
            part = jnp.sum(p * dp, axis=0, keepdims=True)
            dots = part if dots is None else dots + part
        dq = None
        for b in range(3):
            window = rows((c + b) * CHUNK, CHUNK)
            ds = (probs[c, b] * (dprobs[b] - dots)).astype(jnp.bfloat16)
            dk_acc[window, :] += jnp.dot(ds, queries, preferred_element_type=jnp.float32)
            part = jnp.dot(kt[c + b], ds, preferred_element_type=jnp.float32)
            dq = part if dq is None else dq + part
        dq_out[rows(c * CHUNK, CHUNK), :] = (dq * SCALE).T.astype(jnp.bfloat16)

    outputs = {DQ: (dq_out, dq_hbm), DK: (dk_out, dk_hbm), DV: (dv_out, dv_hbm)}

    def local_out(a):
        src, dst = outputs[a]
        return pltpu.make_async_copy(
            src.at[rows(me * ROWS, ROWS)], dst.at[:, rows(me * HEAD_DIM, HEAD_DIM)], recv_sem.at[a, me]
        )

    def remote_out(a, to, source):
        src, dst = outputs[a]
        return pltpu.make_async_remote_copy(
            src.at[rows(to * ROWS, ROWS)],
            dst.at[:, rows(source * HEAD_DIM, HEAD_DIM)],
            send_sem.at[a, to],
            recv_sem.at[a, source],
            device_id=(s, to),
            device_id_type=MESH,
        )

    def send_out(a, c):
        for d in range(2):
            to = c * 2 + d

            @pl.when(to == me)
            def _():
                local_out(a).start()

            @pl.when(to != me)
            def _():
                remote_out(a, to, me).start()

    for o in range(8):
        wait_in(G, o)

    @pl.loop(0, CHUNKS)
    def _(o):
        c = partner_chip(o)
        gradients(c)
        send_out(DQ, c)

    def back(i, src, dst):
        return pltpu.make_async_remote_copy(
            src.at[pl.ds(CHUNKS * CHUNK, HALO * CHUNK)],
            dst,
            hs_sem.at[2 + i],
            hr_sem.at[2 + i],
            device_id=(s - 1, me),
            device_id_type=MESH,
        )

    tail = pl.ds(CHUNKS * CHUNK, HALO * CHUNK)

    @pl.when(jnp.logical_not(first))
    def _():
        dk_out[tail, :] = (dk_acc[: HALO * CHUNK] * SCALE).astype(jnp.bfloat16)
        dv_out[tail, :] = dv_acc[: HALO * CHUNK].astype(jnp.bfloat16)
        back(0, dk_out, part_k).start()
        back(1, dv_out, part_v).start()

    @pl.loop(0, 6)
    def _(i):
        c = (chip + i) % 6
        src = rows((c + HALO) * CHUNK, CHUNK)
        dst = rows(c * CHUNK, CHUNK)
        dv_out[dst, :] = dv_acc[src, :].astype(jnp.bfloat16)
        send_out(DV, c)
        dk_out[dst, :] = (dk_acc[src, :] * SCALE).astype(jnp.bfloat16)
        send_out(DK, c)

    @pl.when(last)
    def _():
        part_k[...] = zero
        part_v[...] = zero

    @pl.when(jnp.logical_not(last))
    def _():
        back(0, dk_out, part_k).wait_recv()
        back(1, dv_out, part_v).wait_recv()

    @pl.loop(0, HALO)
    def _(i):
        p = (chip + i) % HALO
        c = 6 + p
        src = rows((c + HALO) * CHUNK, CHUNK)
        dst = rows(c * CHUNK, CHUNK)
        term = rows(p * CHUNK, CHUNK)
        dv_out[dst, :] = (dv_acc[src, :] + part_v[term, :].astype(jnp.float32)).astype(jnp.bfloat16)
        send_out(DV, c)
        dk_out[dst, :] = (dk_acc[src, :] * SCALE + part_k[term, :].astype(jnp.float32)).astype(jnp.bfloat16)
        send_out(DK, c)

    for a in (K, V, Q, G):
        for o, d in others:
            remote_in(a, device(o, d), me).wait_send()

    @pl.when(jnp.logical_not(last))
    def _():
        halo(0, kbuf).wait_send()
        halo(1, vbuf).wait_send()

    @pl.when(jnp.logical_not(first))
    def _():
        back(0, dk_out, part_k).wait_send()
        back(1, dv_out, part_v).wait_send()

    for a in (DQ, DK, DV):
        local_out(a).wait()
        for o, d in others:
            remote_out(a, device(o, d), me).wait_send()
            remote_out(a, me, device(o, d)).wait_recv()


def per_device(queries, key_vectors, value_vectors, grad_output):
    tokens, width = queries.shape
    bf16, f32 = jnp.bfloat16, jnp.float32
    own, wide = CHUNKS * CHUNK, (CHUNKS + HALO) * CHUNK
    out = jax.ShapeDtypeStruct((tokens, width), bf16)
    anywhere = pl.BlockSpec(memory_space=pl.ANY)
    return pl.pallas_call(
        kernel,
        out_shape=(out, out, out),
        in_specs=[anywhere] * 4,
        out_specs=(anywhere,) * 3,
        scratch_shapes=[
            pltpu.VMEM((wide, HEAD_DIM), bf16),
            pltpu.VMEM((wide, HEAD_DIM), bf16),
            pltpu.VMEM((own, HEAD_DIM), bf16),
            pltpu.VMEM((own, HEAD_DIM), bf16),
            pltpu.VMEM((CHUNKS + HALO, HEAD_DIM, CHUNK), bf16),
            pltpu.VMEM((CHUNKS, 3, CHUNK, CHUNK), f32),
            pltpu.VMEM((3, CHUNK, CHUNK), f32),
            pltpu.VMEM((wide, HEAD_DIM), f32),
            pltpu.VMEM((wide, HEAD_DIM), f32),
            pltpu.VMEM((own, HEAD_DIM), bf16),
            pltpu.VMEM((wide, HEAD_DIM), bf16),
            pltpu.VMEM((wide, HEAD_DIM), bf16),
            pltpu.VMEM((HALO * CHUNK, HEAD_DIM), bf16),
            pltpu.VMEM((HALO * CHUNK, HEAD_DIM), bf16),
            pltpu.SemaphoreType.DMA((7, 16)),
            pltpu.SemaphoreType.DMA((7, 16)),
            pltpu.SemaphoreType.DMA((4,)),
            pltpu.SemaphoreType.DMA((4,)),
        ],
        compiler_params=pltpu.CompilerParams(
            collective_id=0, has_side_effects=True, vmem_limit_bytes=48 * 1024 * 1024
        ),
        name="window_attention_backward",
    )(queries, key_vectors, value_vectors, grad_output)


def solution(mesh):
    placed = P(("seq", "head"), None)
    return jax.shard_map(
        per_device,
        mesh=mesh,
        in_specs=(placed,) * 4,
        out_specs=(placed,) * 3,
        check_vma=False,
    )
```

```python
import functools

import jax
import jax.numpy as jnp
from jax import lax
from jax.experimental import pallas as pl
from jax.experimental.pallas import tpu as pltpu
from jax.sharding import PartitionSpec as P

HEAD_DIM = 128
CHUNK = 256
CHUNKS = 8
HALO = 2
RING = 16
ROWS = 128
SCALE = HEAD_DIM ** (-0.5)
LOG2E = 1.4426950408889634
NEG = -1e30
MESH = pl.DeviceIdType.MESH
K, V, Q, G, DQ, DK, DV = range(7)
NT = (((1,), (1,)), ((), ()))


def kernel(
    q_hbm, k_hbm, v_hbm, g_hbm,
    dq_hbm, dk_hbm, dv_hbm,
    kbuf, vbuf, qbuf, gbuf, kt, probs, dprobs,
    dk_acc, dv_acc, dq_out, dk_out, dv_out, part_k, part_v,
    send_sem, recv_sem, hs_sem, hr_sem, late_sem, next_sem, prev_sem,
):
    s = lax.axis_index("seq")
    me = lax.axis_index("head")
    blocks = lax.axis_size("seq")
    chip, core = me // 2, me % 2
    cx, cy = chip // 2, chip % 2
    first = s == 0
    last = s == blocks - 1

    def partner_chip(o):
        return ((cx + o // 2) % 4) * 2 + (cy + o) % 2

    others = [(o, d) for o in range(8) for d in range(2) if (o, d) != (0, 0)]

    def device(o, d):
        return partner_chip(o) * 2 + (core + d) % 2

    late = first & (me == 0)
    with_late = first & (me != 0)
    starts = s % RING == 0
    ends = (s + 1) % RING == 0
    has_prev, has_next = jnp.logical_not(first), jnp.logical_not(last)

    def signal(sem, block, head):
        pl.semaphore_signal(sem, inc=1, device_id=(block, head), device_id_type=MESH)

    barrier = pltpu.get_barrier_semaphore()

    @pl.when(jnp.logical_not(late))
    def _():
        for o, d in others:
            signal(barrier, s, device(o, d))

    @pl.when(has_next & jnp.logical_not(ends))
    def _():
        signal(barrier, s + 1, me)

    @pl.when(has_prev & starts)
    def _():
        signal(barrier, s - 1, me)

    inputs = {K: (k_hbm, kbuf, HALO * CHUNK), V: (v_hbm, vbuf, HALO * CHUNK), Q: (q_hbm, qbuf, 0), G: (g_hbm, gbuf, 0)}

    def rows(start, size):
        return pl.ds(pl.multiple_of(start, ROWS), size)

    def local_in(a):
        src, dst, base = inputs[a]
        return pltpu.make_async_copy(
            src.at[:, rows(me * ROWS, HEAD_DIM)], dst.at[rows(base + me * ROWS, ROWS)], recv_sem.at[a, me]
        )

    def remote_in(a, to, source):
        src, dst, base = inputs[a]
        return pltpu.make_async_remote_copy(
            src.at[:, rows(to * HEAD_DIM, HEAD_DIM)],
            dst.at[rows(base + source * ROWS, ROWS)],
            send_sem.at[a, to],
            recv_sem.at[a, source],
            device_id=(s, to),
            device_id_type=MESH,
        )

    for a in (K, V, Q, G):
        local_in(a).start()

    zero = jnp.zeros((HALO * CHUNK, HEAD_DIM), jnp.bfloat16)

    @pl.when(first)
    def _():
        kbuf[: HALO * CHUNK] = zero
        vbuf[: HALO * CHUNK] = zero

    dk_acc[...] = jnp.zeros_like(dk_acc)
    dv_acc[...] = jnp.zeros_like(dv_acc)

    count = 15 - with_late.astype(jnp.int32) + jnp.logical_not(starts).astype(jnp.int32)
    count = count + (has_next & ends).astype(jnp.int32)
    pl.semaphore_wait(barrier, count)

    @pl.when(late)
    def _():
        for o, d in others:
            signal(late_sem, s, device(o, d))

    @pl.when(has_prev & jnp.logical_not(starts))
    def _():
        signal(next_sem, s - 1, me)

    @pl.when(has_next & ends)
    def _():
        signal(prev_sem, s + 1, me)

    for a in (K, V, Q, G):
        for o, d in others:
            to = device(o, d)

            @pl.when(jnp.logical_not(first & (to == 0)))
            def _():
                remote_in(a, to, me).start()

    @pl.when(with_late)
    def _():
        pl.semaphore_wait(late_sem, 1)
        for a in (K, V, Q, G):
            remote_in(a, 0, me).start()

    def wait_in(a, c):
        src, dst, base = inputs[a]
        for d in range(2):
            head = c * 2 + d
            pltpu.make_async_copy(
                src.at[:, rows(me * ROWS, HEAD_DIM)], dst.at[rows(base + head * ROWS, ROWS)], recv_sem.at[a, head]
            ).wait()

    def halo(i, buf):
        return pltpu.make_async_remote_copy(
            buf.at[pl.ds(CHUNKS * CHUNK, HALO * CHUNK)],
            buf.at[pl.ds(0, HALO * CHUNK)],
            hs_sem.at[i],
            hr_sem.at[i],
            device_id=(s + 1, me),
            device_id_type=MESH,
        )

    for i, (a, buf) in enumerate(((K, kbuf), (V, vbuf))):
        for c in range(CHUNKS):
            wait_in(a, c)

        if a == K:

            @pl.when(has_next & jnp.logical_not(ends))
            def _():
                pl.semaphore_wait(next_sem, 1)

        @pl.when(has_next)
        def _():
            halo(i, buf).start()

        if a == K:

            @pl.loop(HALO, HALO + CHUNKS)
            def _(b):
                kt[b] = kbuf[rows(b * CHUNK, CHUNK), :].T

    @pl.when(has_prev)
    def _():
        halo(0, kbuf).wait_recv()

    for b in range(HALO):
        kt[b] = kbuf[b * CHUNK : (b + 1) * CHUNK, :].T

    key_ids = lax.broadcasted_iota(jnp.int32, (CHUNK, CHUNK), 0)
    query_ids = lax.broadcasted_iota(jnp.int32, (CHUNK, CHUNK), 1)

    def softmax(c):
        queries = qbuf[rows(c * CHUNK, CHUNK), :]
        top = None
        for b in range(3):
            scores = lax.dot_general(
                kbuf[rows((c + b) * CHUNK, CHUNK), :], queries, NT, preferred_element_type=jnp.float32
            )
            if b == 0:
                scores = jnp.where(key_ids > query_ids, scores, NEG)
            if b == 2:
                scores = jnp.where(key_ids <= query_ids, scores, NEG)
            if b < 2:
                scores = scores + jnp.where(first & (c + b < HALO), NEG, 0.0)
            probs[c, b] = scores
            best = jnp.max(scores, axis=0, keepdims=True)
            top = best if top is None else jnp.maximum(top, best)
        total = None
        for b in range(3):
            e = jnp.exp2((probs[c, b] - top) * (SCALE * LOG2E))
            probs[c, b] = e
            part = jnp.sum(e, axis=0, keepdims=True)
            total = part if total is None else total + part
        inverse = 1.0 / total
        for b in range(3):
            probs[c, b] = probs[c, b] * inverse

    @pl.loop(0, CHUNKS)
    def _(i):
        c = (chip + i) % CHUNKS
        wait_in(Q, c)
        softmax(c)

    @pl.when(has_prev)
    def _():
        halo(1, vbuf).wait_recv()

    def gradients(c):
        queries = qbuf[rows(c * CHUNK, CHUNK), :]
        grads = gbuf[rows(c * CHUNK, CHUNK), :]
        dots = None
        for b in range(3):
            window = rows((c + b) * CHUNK, CHUNK)
            p = probs[c, b]
            dv_acc[window, :] += jnp.dot(p.astype(jnp.bfloat16), grads, preferred_element_type=jnp.float32)
            dp = lax.dot_general(vbuf[window, :], grads, NT, preferred_element_type=jnp.float32)
            dprobs[b] = dp
            part = jnp.sum(p * dp, axis=0, keepdims=True)
            dots = part if dots is None else dots + part
        dq = None
        for b in range(3):
            window = rows((c + b) * CHUNK, CHUNK)
            ds = (probs[c, b] * (dprobs[b] - dots)).astype(jnp.bfloat16)
            dk_acc[window, :] += jnp.dot(ds, queries, preferred_element_type=jnp.float32)
            part = jnp.dot(kt[c + b], ds, preferred_element_type=jnp.float32)
            dq = part if dq is None else dq + part
        dq_out[rows(c * CHUNK, CHUNK), :] = (dq * SCALE).T.astype(jnp.bfloat16)

    outputs = {DQ: (dq_out, dq_hbm), DK: (dk_out, dk_hbm), DV: (dv_out, dv_hbm)}

    def local_out(a):
        src, dst = outputs[a]
        return pltpu.make_async_copy(
            src.at[rows(me * ROWS, ROWS)], dst.at[:, rows(me * HEAD_DIM, HEAD_DIM)], recv_sem.at[a, me]
        )

    def remote_out(a, to, source):
        src, dst = outputs[a]
        return pltpu.make_async_remote_copy(
            src.at[rows(to * ROWS, ROWS)],
            dst.at[:, rows(source * HEAD_DIM, HEAD_DIM)],
            send_sem.at[a, to],
            recv_sem.at[a, source],
            device_id=(s, to),
            device_id_type=MESH,
        )

    def send_out(a, c):
        for d in range(2):
            to = c * 2 + d

            @pl.when(to == me)
            def _():
                local_out(a).start()

            @pl.when(to != me)
            def _():
                remote_out(a, to, me).start()

    def back(i, src, dst):
        return pltpu.make_async_remote_copy(
            src.at[pl.ds(CHUNKS * CHUNK, HALO * CHUNK)],
            dst,
            hs_sem.at[2 + i],
            hr_sem.at[2 + i],
            device_id=(s - 1, me),
            device_id_type=MESH,
        )

    tail = pl.ds(CHUNKS * CHUNK, HALO * CHUNK)

    @pl.when(has_prev & starts)
    def _():
        pl.semaphore_wait(prev_sem, 1)

    @pl.loop(0, CHUNKS)
    def _(i):
        c = jnp.where(i < HALO, i, HALO + (chip + i) % (CHUNKS - HALO))
        wait_in(G, c)
        gradients(c)
        send_out(DQ, c)

        @pl.when(has_prev & (i == HALO - 1))
        def _():
            dv_out[tail, :] = dv_acc[: HALO * CHUNK].astype(jnp.bfloat16)
            back(1, dv_out, part_v).start()
            dk_out[tail, :] = (dk_acc[: HALO * CHUNK] * SCALE).astype(jnp.bfloat16)
            back(0, dk_out, part_k).start()

    @pl.loop(0, 6)
    def _(i):
        c = (chip + i) % 6
        src = rows((c + HALO) * CHUNK, CHUNK)
        dst = rows(c * CHUNK, CHUNK)
        dv_out[dst, :] = dv_acc[src, :].astype(jnp.bfloat16)
        send_out(DV, c)
        dk_out[dst, :] = (dk_acc[src, :] * SCALE).astype(jnp.bfloat16)
        send_out(DK, c)

    @pl.when(last)
    def _():
        part_k[...] = zero
        part_v[...] = zero

    @pl.when(has_next)
    def _():
        back(0, dk_out, part_k).wait_recv()
        back(1, dv_out, part_v).wait_recv()

    @pl.loop(0, HALO)
    def _(i):
        p = (chip + i) % HALO
        c = 6 + p
        src = rows((c + HALO) * CHUNK, CHUNK)
        dst = rows(c * CHUNK, CHUNK)
        term = rows(p * CHUNK, CHUNK)
        dv_out[dst, :] = (dv_acc[src, :] + part_v[term, :].astype(jnp.float32)).astype(jnp.bfloat16)
        send_out(DV, c)
        dk_out[dst, :] = (dk_acc[src, :] * SCALE + part_k[term, :].astype(jnp.float32)).astype(jnp.bfloat16)
        send_out(DK, c)

    for a in (K, V, Q, G):
        for o, d in others:
            remote_in(a, device(o, d), me).wait_send()

    @pl.when(has_next)
    def _():
        halo(0, kbuf).wait_send()
        halo(1, vbuf).wait_send()

    @pl.when(has_prev)
    def _():
        back(0, dk_out, part_k).wait_send()
        back(1, dv_out, part_v).wait_send()

    for a in (DQ, DK, DV):
        local_out(a).wait()
        for o, d in others:
            remote_out(a, device(o, d), me).wait_send()
            remote_out(a, me, device(o, d)).wait_recv()


def store(a, b, c, x, y, z, sem):
    copies = [pltpu.make_async_copy(src, dst, sem.at[i]) for i, (src, dst) in enumerate(((a, x), (b, y), (c, z)))]
    for copy in copies:
        copy.start()
    for copy in copies:
        copy.wait()


def per_device(queries, key_vectors, value_vectors, grad_output):
    tokens, width = queries.shape
    bf16, f32 = jnp.bfloat16, jnp.float32
    own, wide = CHUNKS * CHUNK, (CHUNKS + HALO) * CHUNK
    out = jax.ShapeDtypeStruct((tokens, width), bf16)
    anywhere = pl.BlockSpec(memory_space=pl.ANY)
    grads = pl.pallas_call(
        kernel,
        out_shape=(out, out, out),
        in_specs=[anywhere] * 4,
        out_specs=(anywhere,) * 3,
        scratch_shapes=[
            pltpu.VMEM((wide, HEAD_DIM), bf16),
            pltpu.VMEM((wide, HEAD_DIM), bf16),
            pltpu.VMEM((own, HEAD_DIM), bf16),
            pltpu.VMEM((own, HEAD_DIM), bf16),
            pltpu.VMEM((CHUNKS + HALO, HEAD_DIM, CHUNK), bf16),
            pltpu.VMEM((CHUNKS, 3, CHUNK, CHUNK), f32),
            pltpu.VMEM((3, CHUNK, CHUNK), f32),
            pltpu.VMEM((wide, HEAD_DIM), f32),
            pltpu.VMEM((wide, HEAD_DIM), f32),
            pltpu.VMEM((own, HEAD_DIM), bf16),
            pltpu.VMEM((wide, HEAD_DIM), bf16),
            pltpu.VMEM((wide, HEAD_DIM), bf16),
            pltpu.VMEM((HALO * CHUNK, HEAD_DIM), bf16),
            pltpu.VMEM((HALO * CHUNK, HEAD_DIM), bf16),
            pltpu.SemaphoreType.DMA((7, 16)),
            pltpu.SemaphoreType.DMA((7, 16)),
            pltpu.SemaphoreType.DMA((4,)),
            pltpu.SemaphoreType.DMA((4,)),
            pltpu.SemaphoreType.REGULAR,
            pltpu.SemaphoreType.REGULAR,
            pltpu.SemaphoreType.REGULAR,
        ],
        compiler_params=pltpu.CompilerParams(
            collective_id=0, has_side_effects=True, vmem_limit_bytes=52 * 1024 * 1024
        ),
        name="window_attention_backward",
    )(queries, key_vectors, value_vectors, grad_output)
    return pl.pallas_call(
        store,
        out_shape=(out, out, out),
        in_specs=[anywhere] * 3,
        out_specs=(anywhere,) * 3,
        scratch_shapes=[pltpu.SemaphoreType.DMA((3,))],
        compiler_params=pltpu.CompilerParams(vmem_limit_bytes=8 * 1024 * 1024),
        name="store",
    )(*grads)


def solution(mesh):
    placed = P(("seq", "head"), None)
    return jax.shard_map(
        per_device,
        mesh=mesh,
        in_specs=(placed,) * 4,
        out_specs=(placed,) * 3,
        check_vma=False,
    )
```

```python
import functools

import jax
import jax.numpy as jnp
from jax import lax
from jax.experimental import pallas as pl
from jax.experimental.pallas import tpu as pltpu
from jax.sharding import PartitionSpec as P

HEAD_DIM = 128
CHUNK = 256
CHUNKS = 8
HALO = 2
RING = 16
ORDER = (0, 5, 3, 7, 1, 4, 2, 6)
EARLY = 3
LATE_PLACE = 5
RELAYS = (RING, RING, RING + 1, RING + 2)
DIRECT = 2
ORDER_HALO = (5, 3, 7, 1, 0, 4, 2, 6)
ROWS = 128
SCALE = HEAD_DIM ** (-0.5)
LOG2E = 1.4426950408889634
NEG = -1e30
MESH = pl.DeviceIdType.MESH
K, V, Q, G, DQ, DK, DV = range(7)
NT = (((1,), (1,)), ((), ()))


def kernel(
    q_hbm, k_hbm, v_hbm, g_hbm,
    dq_hbm, dk_hbm, dv_hbm,
    kbuf, vbuf, qbuf, gbuf, kt, probs, dprobs,
    dk_acc, dv_acc, dq_out, dk_out, dv_out, part_k, part_v,
    relay,
    send_sem, recv_sem, hs_sem, hr_sem, turn_send, turn_recv, relay_send, relay_recv, late_sem, next_sem, prev_sem,
):
    s = lax.axis_index("seq")
    me = lax.axis_index("head")
    blocks = lax.axis_size("seq")
    chip, core = me // 2, me % 2
    cx, cy = chip // 2, chip % 2
    first = s == 0
    last = s == blocks - 1

    def partner_chip(o):
        return ((cx + o // 2) % 4) * 2 + (cy + o) % 2

    others = [(o, d) for o in ORDER for d in range(2) if (o, d) != (0, 0)]

    def device(o, d):
        return partner_chip(o) * 2 + (core + d) % 2

    late = first & (me == 0)
    with_late = first & (me != 0)
    starts = s % RING == 0
    ends = (s + 1) % RING == 0
    has_prev, has_next = jnp.logical_not(first), jnp.logical_not(last)
    turn_to, turn_from = has_prev & starts, has_next & ends
    relays, far_relay, slot = False, s == RING + 2, 0
    for n in range(DIRECT, len(RELAYS)):
        relays = relays | (s == RELAYS[n])
        slot = jnp.where(s == RELAYS[n], n, slot)

    def signal(sem, block, head):
        pl.semaphore_signal(sem, inc=1, device_id=(block, head), device_id_type=MESH)

    barrier = pltpu.get_barrier_semaphore()

    @pl.when(jnp.logical_not(late))
    def _():
        for o, d in others:
            signal(barrier, s, device(o, d))

    @pl.when(has_next & jnp.logical_not(ends))
    def _():
        signal(barrier, s + 1, me)

    @pl.when(turn_to)
    def _():
        signal(barrier, s - 1, me)
        signal(barrier, RING + 2, me)

    @pl.when(relays)
    def _():
        signal(barrier, RING - 1, me)

    inputs = {K: (k_hbm, kbuf, HALO * CHUNK), V: (v_hbm, vbuf, HALO * CHUNK), Q: (q_hbm, qbuf, 0), G: (g_hbm, gbuf, 0)}

    def rows(start, size):
        return pl.ds(pl.multiple_of(start, ROWS), size)

    def local_in(a):
        src, dst, base = inputs[a]
        return pltpu.make_async_copy(
            src.at[:, rows(me * ROWS, HEAD_DIM)], dst.at[rows(base + me * ROWS, ROWS)], recv_sem.at[a, me]
        )

    def remote_in(a, to, source):
        src, dst, base = inputs[a]
        return pltpu.make_async_remote_copy(
            src.at[:, rows(to * HEAD_DIM, HEAD_DIM)],
            dst.at[rows(base + source * ROWS, ROWS)],
            send_sem.at[a, to],
            recv_sem.at[a, source],
            device_id=(s, to),
            device_id_type=MESH,
        )

    for a in (K, V, Q, G):
        local_in(a).start()

    zero = jnp.zeros((HALO * CHUNK, HEAD_DIM), jnp.bfloat16)

    @pl.when(first)
    def _():
        kbuf[: HALO * CHUNK] = zero
        vbuf[: HALO * CHUNK] = zero

    dk_acc[...] = jnp.zeros_like(dk_acc)
    dv_acc[...] = jnp.zeros_like(dv_acc)

    count = 15 - with_late.astype(jnp.int32) + jnp.logical_not(starts).astype(jnp.int32)
    count = count + turn_from.astype(jnp.int32) * (1 + len(RELAYS) - DIRECT) + far_relay.astype(jnp.int32)
    pl.semaphore_wait(barrier, count)

    @pl.when(late)
    def _():
        for o, d in others:
            signal(late_sem, s, device(o, d))

    @pl.when(has_prev & jnp.logical_not(starts))
    def _():
        signal(next_sem, s - 1, me)

    @pl.when(has_next & ends)
    def _():
        signal(prev_sem, s + 1, me)

    for group in ((K,), (V,)):
        for o, d in others:
            to = device(o, d)

            @pl.when(jnp.logical_not(first & (to == 0)))
            def _():
                for a in group:
                    remote_in(a, to, me).start()

    @pl.when(with_late)
    def _():
        pl.semaphore_wait(late_sem, 1)
        for a in (K, V):
            remote_in(a, 0, me).start()

    for a in (Q, G):
        for o, d in others:
            remote_in(a, device(o, d), me).start()

    def wait_in(a, c):
        src, dst, base = inputs[a]
        for d in range(2):
            head = c * 2 + d
            pltpu.make_async_copy(
                src.at[:, rows(me * ROWS, HEAD_DIM)], dst.at[rows(base + head * ROWS, ROWS)], recv_sem.at[a, head]
            ).wait()

    def halo(i, buf):
        return pltpu.make_async_remote_copy(
            buf.at[pl.ds(CHUNKS * CHUNK, HALO * CHUNK)],
            buf.at[pl.ds(0, HALO * CHUNK)],
            hs_sem.at[i],
            hr_sem.at[i],
            device_id=(s + 1, me),
            device_id_type=MESH,
        )

    def piece(i, n):
        buf = (kbuf, vbuf)[i]
        return pltpu.make_async_remote_copy(
            buf.at[pl.ds(CHUNKS * CHUNK + n * ROWS, ROWS)],
            buf.at[pl.ds(n * ROWS, ROWS)] if n < DIRECT else relay.at[i],
            turn_send.at[i, n],
            turn_recv.at[i, n] if n < DIRECT else relay_recv.at[i],
            device_id=(RELAYS[n], me),
            device_id_type=MESH,
        )

    def forward(i):
        return pltpu.make_async_remote_copy(
            relay.at[i],
            (kbuf, vbuf)[i].at[rows(slot * ROWS, ROWS)],
            relay_send.at[i],
            turn_recv.at[i, slot],
            device_id=(RING, me),
            device_id_type=MESH,
        )

    def wait_piece(i, n):
        buf = (kbuf, vbuf)[i]
        pltpu.make_async_copy(
            buf.at[pl.ds(CHUNKS * CHUNK, ROWS)], buf.at[pl.ds(n * ROWS, ROWS)], turn_recv.at[i, n]
        ).wait()

    def pass_on(i):
        pltpu.make_async_copy(relay.at[i], relay.at[i], relay_recv.at[i]).wait()
        forward(i).start()

    for i, (a, buf) in enumerate(((K, kbuf), (V, vbuf))):
        for c in range(CHUNKS - HALO, CHUNKS):
            wait_in(a, c)

        if a == K:

            @pl.when(has_next & jnp.logical_not(ends))
            def _():
                pl.semaphore_wait(next_sem, 1)

        @pl.when(has_next & jnp.logical_not(ends))
        def _():
            halo(i, buf).start()

        @pl.when(turn_from)
        def _():
            for n in range(len(RELAYS)):
                piece(i, n).start()

        for c in range(CHUNKS - HALO):
            wait_in(a, c)

        if a == K:

            @pl.loop(HALO, HALO + CHUNKS)
            def _(b):
                kt[b] = kbuf[rows(b * CHUNK, CHUNK), :].T

    key_ids = lax.broadcasted_iota(jnp.int32, (CHUNK, CHUNK), 0)
    query_ids = lax.broadcasted_iota(jnp.int32, (CHUNK, CHUNK), 1)

    def softmax(c):
        queries = qbuf[rows(c * CHUNK, CHUNK), :]
        top = None
        for b in range(3):
            scores = lax.dot_general(
                kbuf[rows((c + b) * CHUNK, CHUNK), :], queries, NT, preferred_element_type=jnp.float32
            )
            if b == 0:
                scores = jnp.where(key_ids > query_ids, scores, NEG)
            if b == 2:
                scores = jnp.where(key_ids <= query_ids, scores, NEG)
            if b < 2:
                scores = scores + jnp.where(first & (c + b < HALO), NEG, 0.0)
            probs[c, b] = scores
            best = jnp.max(scores, axis=0, keepdims=True)
            top = best if top is None else jnp.maximum(top, best)
        total = None
        for b in range(3):
            e = jnp.exp2((probs[c, b] - top) * (SCALE * LOG2E))
            probs[c, b] = e
            part = jnp.sum(e, axis=0, keepdims=True)
            total = part if total is None else total + part
        inverse = 1.0 / total
        for b in range(3):
            probs[c, b] = probs[c, b] * inverse

    def gradients(c):
        queries = qbuf[rows(c * CHUNK, CHUNK), :]
        grads = gbuf[rows(c * CHUNK, CHUNK), :]
        dots = None
        for b in range(3):
            window = rows((c + b) * CHUNK, CHUNK)
            p = probs[c, b]
            dv_acc[window, :] += jnp.dot(p.astype(jnp.bfloat16), grads, preferred_element_type=jnp.float32)
            dp = lax.dot_general(vbuf[window, :], grads, NT, preferred_element_type=jnp.float32)
            dprobs[b] = dp
            part = jnp.sum(p * dp, axis=0, keepdims=True)
            dots = part if dots is None else dots + part
        dq = None
        for b in range(3):
            window = rows((c + b) * CHUNK, CHUNK)
            ds = (probs[c, b] * (dprobs[b] - dots)).astype(jnp.bfloat16)
            dk_acc[window, :] += jnp.dot(ds, queries, preferred_element_type=jnp.float32)
            part = jnp.dot(kt[c + b], ds, preferred_element_type=jnp.float32)
            dq = part if dq is None else dq + part
        dq_out[rows(c * CHUNK, CHUNK), :] = (dq * SCALE).T.astype(jnp.bfloat16)

    outputs = {DQ: (dq_out, dq_hbm), DK: (dk_out, dk_hbm), DV: (dv_out, dv_hbm)}

    def local_out(a):
        src, dst = outputs[a]
        return pltpu.make_async_copy(
            src.at[rows(me * ROWS, ROWS)], dst.at[:, rows(me * HEAD_DIM, HEAD_DIM)], recv_sem.at[a, me]
        )

    def remote_out(a, to, source):
        src, dst = outputs[a]
        return pltpu.make_async_remote_copy(
            src.at[rows(to * ROWS, ROWS)],
            dst.at[:, rows(source * HEAD_DIM, HEAD_DIM)],
            send_sem.at[a, to],
            recv_sem.at[a, source],
            device_id=(s, to),
            device_id_type=MESH,
        )

    def send_out(a, c):
        for d in range(2):
            to = c * 2 + d

            @pl.when(to == me)
            def _():
                local_out(a).start()

            @pl.when(to != me)
            def _():
                remote_out(a, to, me).start()

    def back(i, part):
        src, dst = ((dv_out, part_v), (dk_out, part_k))[i]
        return pltpu.make_async_remote_copy(
            src.at[pl.ds((CHUNKS + part) * CHUNK, CHUNK)],
            dst.at[pl.ds(part * CHUNK, CHUNK)],
            hs_sem.at[2 + 2 * part + i],
            hr_sem.at[2 + 2 * part + i],
            device_id=(s - 1, me),
            device_id_type=MESH,
        )

    def send_back(part):
        src, dst = pl.ds(part * CHUNK, CHUNK), pl.ds((CHUNKS + part) * CHUNK, CHUNK)
        dv_out[dst, :] = dv_acc[src, :].astype(jnp.bfloat16)
        back(0, part).start()
        dk_out[dst, :] = (dk_acc[src, :] * SCALE).astype(jnp.bfloat16)
        back(1, part).start()

    def finish(c):
        src = rows((c + HALO) * CHUNK, CHUNK)
        dst = rows(c * CHUNK, CHUNK)
        dv_out[dst, :] = dv_acc[src, :].astype(jnp.bfloat16)
        send_out(DV, c)
        dk_out[dst, :] = (dk_acc[src, :] * SCALE).astype(jnp.bfloat16)
        send_out(DK, c)

    @pl.when(has_prev & starts)
    def _():
        pl.semaphore_wait(prev_sem, 1)

    halo_chip = chip < HALO
    base_order = []
    for n in range(CHUNKS):
        o = jnp.where(halo_chip, ORDER_HALO[n], ORDER[n])
        base_order.append(((cx + 4 - o // 2) % 4) * 2 + (cy + o) % 2)

    def moved(order, chunk, to, condition):
        place = sum(jnp.where(order[n] == chunk, n, 0) for n in range(CHUNKS))
        result = []
        for n in range(CHUNKS):
            after = order[min(n + 1, CHUNKS - 1)]
            value = jnp.where((n >= place) & (n < to), after, jnp.where(n == to, chunk, order[n]))
            result.append(jnp.where(condition & (place < to), value, order[n]))
        return result

    chunk_order = moved(base_order, 0, LATE_PLACE, first)
    turn = turn_to
    chunk_order = moved(chunk_order, 0, 5, turn)
    chunk_order = moved(chunk_order, 1, 5, turn)

    def chunk_at(i):
        c = chunk_order[0]
        for n in range(1, CHUNKS):
            c = jnp.where(i == n, chunk_order[n], c)
        return c

    def wait_halo(a, buf):
        @pl.when(has_prev & jnp.logical_not(starts))
        def _():
            halo(a, buf).wait_recv()

        @pl.when(turn_to)
        def _():
            for n in range(len(RELAYS)):
                wait_piece(a, n)

    def weights(i, met):
        c = chunk_at(i)

        @pl.when(relays & (i == 1))
        def _():
            pass_on(0)

        @pl.when((c < HALO) & (met == 0))
        def _():
            wait_halo(0, kbuf)

            for b in range(HALO):
                kt[b] = kbuf[b * CHUNK : (b + 1) * CHUNK, :].T

        wait_in(Q, c)
        softmax(c)
        return met + (c < HALO).astype(jnp.int32)

    lax.fori_loop(0, CHUNKS, weights, 0)

    limit = EARLY

    def step(i, carry):
        done, sent, total = carry
        c = chunk_at(i)

        @pl.when(relays & (i == 2))
        def _():
            pass_on(1)

        @pl.when((c < HALO) & (done % 4 == 0))
        def _():
            wait_halo(1, vbuf)

        wait_in(G, c)
        gradients(c)
        send_out(DQ, c)
        bit = 1
        for n in range(1, CHUNKS):
            bit = jnp.where(c == n, 2**n, bit)
        done = done + bit

        @pl.when(has_prev & (c == 0))
        def _():
            send_back(0)

        @pl.when(has_prev & (c < HALO) & (done % 4 == 3))
        def _():
            send_back(1)

        for b in range(3):
            key = c - b
            need = 0
            for n in range(CHUNKS - HALO):
                need = jnp.where((key == n) & ((done // 2**n) % 8 == 7) & (total < limit), 2**n, need)

            @pl.when(need > 0)
            def _():
                finish(key)

            sent = sent + need
            total = total + (need > 0).astype(jnp.int32)

        return done, sent, total

    _, sent, _ = lax.fori_loop(0, CHUNKS, step, (0, 0, 0))

    zero_part = jnp.zeros((CHUNK, HEAD_DIM), jnp.bfloat16)
    for part in range(HALO):
        window = pl.ds(part * CHUNK, CHUNK)

        @pl.when(last)
        def _():
            part_k[window, :] = zero_part
            part_v[window, :] = zero_part

        @pl.when(has_next)
        def _():
            back(0, part).wait_recv()
            back(1, part).wait_recv()

        c = CHUNKS - HALO + part
        src = pl.ds((c + HALO) * CHUNK, CHUNK)
        dst = pl.ds(c * CHUNK, CHUNK)
        dv_out[dst, :] = (dv_acc[src, :] + part_v[window, :].astype(jnp.float32)).astype(jnp.bfloat16)
        send_out(DV, c)
        dk_out[dst, :] = (dk_acc[src, :] * SCALE + part_k[window, :].astype(jnp.float32)).astype(jnp.bfloat16)
        send_out(DK, c)

    for n in range(CHUNKS - HALO):

        @pl.when((sent // 2**n) % 2 == 0)
        def _():
            finish(n)

    for a in (K, V, Q, G):
        for o, d in others:
            remote_in(a, device(o, d), me).wait_send()

    @pl.when(has_next & jnp.logical_not(ends))
    def _():
        halo(0, kbuf).wait_send()
        halo(1, vbuf).wait_send()

    @pl.when(turn_from)
    def _():
        for n in range(len(RELAYS)):
            piece(0, n).wait_send()
            piece(1, n).wait_send()

    @pl.when(relays)
    def _():
        forward(0).wait_send()
        forward(1).wait_send()

    @pl.when(has_prev)
    def _():
        for part in range(HALO):
            back(0, part).wait_send()
            back(1, part).wait_send()

    for a in (DQ, DK, DV):
        local_out(a).wait()
        for o, d in others:
            remote_out(a, device(o, d), me).wait_send()
            remote_out(a, me, device(o, d)).wait_recv()


def store(a, b, c, x, y, z, sem):
    copies = [pltpu.make_async_copy(src, dst, sem.at[i]) for i, (src, dst) in enumerate(((a, x), (b, y), (c, z)))]
    for copy in copies:
        copy.start()
    for copy in copies:
        copy.wait()


def per_device(queries, key_vectors, value_vectors, grad_output):
    tokens, width = queries.shape
    bf16, f32 = jnp.bfloat16, jnp.float32
    own, wide = CHUNKS * CHUNK, (CHUNKS + HALO) * CHUNK
    out = jax.ShapeDtypeStruct((tokens, width), bf16)
    anywhere = pl.BlockSpec(memory_space=pl.ANY)
    grads = pl.pallas_call(
        kernel,
        out_shape=(out, out, out),
        in_specs=[anywhere] * 4,
        out_specs=(anywhere,) * 3,
        scratch_shapes=[
            pltpu.VMEM((wide, HEAD_DIM), bf16),
            pltpu.VMEM((wide, HEAD_DIM), bf16),
            pltpu.VMEM((own, HEAD_DIM), bf16),
            pltpu.VMEM((own, HEAD_DIM), bf16),
            pltpu.VMEM((CHUNKS + HALO, HEAD_DIM, CHUNK), bf16),
            pltpu.VMEM((CHUNKS, 3, CHUNK, CHUNK), f32),
            pltpu.VMEM((3, CHUNK, CHUNK), f32),
            pltpu.VMEM((wide, HEAD_DIM), f32),
            pltpu.VMEM((wide, HEAD_DIM), f32),
            pltpu.VMEM((own, HEAD_DIM), bf16),
            pltpu.VMEM((wide, HEAD_DIM), bf16),
            pltpu.VMEM((wide, HEAD_DIM), bf16),
            pltpu.VMEM((HALO * CHUNK, HEAD_DIM), bf16),
            pltpu.VMEM((HALO * CHUNK, HEAD_DIM), bf16),
            pltpu.VMEM((2, ROWS, HEAD_DIM), bf16),
            pltpu.SemaphoreType.DMA((7, 16)),
            pltpu.SemaphoreType.DMA((7, 16)),
            pltpu.SemaphoreType.DMA((6,)),
            pltpu.SemaphoreType.DMA((6,)),
            pltpu.SemaphoreType.DMA((2, len(RELAYS))),
            pltpu.SemaphoreType.DMA((2, len(RELAYS))),
            pltpu.SemaphoreType.DMA((2,)),
            pltpu.SemaphoreType.DMA((2,)),
            pltpu.SemaphoreType.REGULAR,
            pltpu.SemaphoreType.REGULAR,
            pltpu.SemaphoreType.REGULAR,
        ],
        compiler_params=pltpu.CompilerParams(
            collective_id=0, has_side_effects=True, vmem_limit_bytes=52 * 1024 * 1024
        ),
        name="window_attention_backward",
    )(queries, key_vectors, value_vectors, grad_output)
    return pl.pallas_call(
        store,
        out_shape=(out, out, out),
        in_specs=[anywhere] * 3,
        out_specs=(anywhere,) * 3,
        scratch_shapes=[pltpu.SemaphoreType.DMA((3,))],
        compiler_params=pltpu.CompilerParams(vmem_limit_bytes=8 * 1024 * 1024),
        name="store",
    )(*grads)


def solution(mesh):
    placed = P(("seq", "head"), None)
    return jax.shard_map(
        per_device,
        mesh=mesh,
        in_specs=(placed,) * 4,
        out_specs=(placed,) * 3,
        check_vma=False,
    )
```
